32 devices in a mesh: dp: 4 (over y, x), mp: 8 (over z, core).
Axes of the slice: x: 2, y: 2, z: 4, core: 2. Of those that a mesh axis runs over, the one named last changes fastest.
Arguments:
- inputs: bfloat16 [8, 256, 6144], P('dp', None, 'mp'), may hold values from -6 to 6
- cotangent: bfloat16 [8, 256, 6144], P('dp', None, 'mp'), may hold values from -6 to 6
- w_up: bfloat16 [6144, 24576], P('dp', 'mp'), may hold values from -0.078125 to 0.078125
- w_down: bfloat16 [24576, 6144], P('mp', 'dp'), may hold values from -0.0390625 to 0.0390625
- thresholds: float32 [2], replicated, may hold values from 23592.96 to 58982.4
Outputs:
- grad_up: float32 [6144, 24576], P('dp', 'mp')
- grad_down: float32 [24576, 6144], P('mp', 'dp')
- norms: float32 [8, 2], P('dp')
The draws below stay inside these ranges and needn't reach their ends.
All inputs are finite; a program needn't handle non-finite values.
Results may differ from the reference program's by a relative error of at most 0.0085.
Values may be sent and summed in bfloat16 or wider, within the bound.
No kernel may reach another device: no remote copies, remote signals or barrier semaphores. Data moves between devices by JAX's collectives and lax.ppermute only.
A program may use at most 256 MiB of HBM per device.

```python
import math
import jax
import jax.numpy as jnp
from jax import lax

D = 6144
FF = 24576
P_SIZE = 256
IMG_DEV = 2
IMAGES = 8
N_DP = 4


def patch_field(key, window):
    random_part = jax.random.normal(key, (IMAGES, P_SIZE, D), jnp.float32)
    summed = jnp.zeros((IMAGES, P_SIZE, D), jnp.float32)
    for offset in range(window):
        summed = summed + jnp.roll(random_part, offset, axis=1)
    return summed / math.sqrt(window)


def drawn_field(key):
    key_base, key_smooth = jax.random.split(key)
    rough_part = jax.random.normal(key_base, (IMAGES, P_SIZE, D), jnp.float32)
    smooth = patch_field(key_smooth, max(2, P_SIZE // 16))
    return jnp.clip(0.7071 * rough_part + 0.7071 * smooth, -6.0, 6.0)


def draw_inputs(key, part):
    field_key = jax.random.fold_in(key, 29)
    blended = drawn_field(field_key)
    return blended.astype(jnp.bfloat16)


def draw_cotangent(key, part):
    key_field, key_order, key_jitter = jax.random.split(jax.random.fold_in(key, 17), 3)
    ranking = jax.random.permutation(key_order, IMAGES).astype(jnp.float32)
    jitter = jax.random.uniform(key_jitter, (IMAGES,), jnp.float32, 0.0, 1.0)
    scales = jnp.exp(math.log(0.05) + (ranking + jitter) / IMAGES * math.log(20.0)).reshape(IMAGES, 1, 1)
    blended = drawn_field(key_field)
    return (blended * scales).astype(jnp.bfloat16)


def steps_of(key, dims, cuts, smallest, high):
    factor_of, own = 1.0, jax.random.fold_in(key, 6)
    for axis_at, shards_of in cuts:
        steps = jnp.exp(jax.random.uniform(jax.random.fold_in(own, axis_at), (shards_of,), jnp.float32, smallest / len(cuts), high / len(cuts)))
        factor_of = factor_of * jnp.repeat(steps, dims[axis_at] // shards_of).reshape([-1 if axis == axis_at else 1 for axis in range(len(dims))])
    return factor_of


def gaussian(key, shape, scale, bound, cuts=(), dtype=jnp.bfloat16):
    values = jax.random.normal(key, shape, jnp.float32) * scale
    if len(cuts) > 0:
        values = steps_of(key, shape, cuts, -0.22, 0.18) * values
    return jnp.clip(values, min=-bound, max=bound).astype(dtype)


def setup_inputs(seed: int = 0) -> dict:
    streams_of = jax.random.split(jax.random.key(seed), 6)
    inputs = draw_inputs(jax.random.fold_in(streams_of[5], 71), 0)
    cotangent = draw_cotangent(jax.random.fold_in(streams_of[5], 71), 0)
    w_up = gaussian(streams_of[2], (D, FF), D ** -0.5, 0.078125, ((0, 4), (1, 8)))
    w_down = gaussian(streams_of[3], (FF, D), FF ** -0.5, 0.0390625, ((0, 8), (1, 4)))
    thresholds = jnp.clip(jnp.exp(jax.random.uniform(streams_of[4], (2,), jnp.float32, math.log(23592.96), math.log(58982.4))), 23592.96, 58982.4)
    return {"inputs": inputs, "cotangent": cotangent, "w_up": w_up, "w_down": w_down, "thresholds": thresholds}


inv_root_two = 0.7071067811865476
inv_root_two_pi = 0.3989422804014327

def normal_cdf(value):
    return 0.5 * (1.0 + lax.erf(value * inv_root_two))

def gram_of(array):
    cube = array.reshape(IMAGES, P_SIZE, -1).astype(jnp.float32)
    return jnp.einsum('btd,bsd->bts', cube, cube, precision=lax.Precision.HIGHEST)

def group_sum(left, right):
    left_groups = left.reshape(N_DP, IMG_DEV * P_SIZE, left.shape[1])
    right_groups = right.reshape(N_DP, IMG_DEV * P_SIZE, right.shape[1])

    def add_group(total, pair):
        term = lax.dot_general(pair[0], pair[1], (((0,), (0,)), ((), ())), preferred_element_type=jnp.float32)
        rounded = lax.optimization_barrier(term.astype(jnp.bfloat16))
        return (total + rounded.astype(jnp.float32), None)
    start = jnp.zeros((left.shape[1], right.shape[1]), jnp.float32)
    total, _ = lax.scan(add_group, start, (left_groups, right_groups))
    return total

def reference(inputs, cotangent, w_up, w_down, thresholds):
    rows = inputs.reshape(IMAGES * P_SIZE, D)
    dy_rows = cotangent.reshape(IMAGES * P_SIZE, D)
    pre = jnp.dot(rows, w_up, preferred_element_type=jnp.float32)
    act = (pre * normal_cdf(pre)).astype(jnp.bfloat16)
    dact = jnp.dot(dy_rows, w_down.T, preferred_element_type=jnp.float32)
    slope = normal_cdf(pre) + pre * jnp.exp(-0.5 * pre * pre) * inv_root_two_pi
    dpre = (dact * slope).astype(jnp.bfloat16)
    sq_up = lax.optimization_barrier(jnp.sum(gram_of(rows) * gram_of(dpre), axis=(1, 2)))
    sq_down = lax.optimization_barrier(jnp.sum(gram_of(act) * gram_of(dy_rows), axis=(1, 2)))
    norms = jnp.stack([jnp.sqrt(sq_up), jnp.sqrt(sq_down)], axis=1)
    factor = jnp.minimum(1.0, thresholds[None, :] / (norms + 1e-06))
    dpre_clip = (factor[:, 0][:, None, None] * dpre.reshape(IMAGES, P_SIZE, FF).astype(jnp.float32)).astype(jnp.bfloat16).reshape(IMAGES * P_SIZE, FF)
    cot_clip = (factor[:, 1][:, None, None] * cotangent.astype(jnp.float32)).astype(jnp.bfloat16).reshape(IMAGES * P_SIZE, D)
    grad_up = group_sum(rows, dpre_clip)
    grad_down = group_sum(act, cot_clip)
    return (grad_up, grad_down, norms)
```

```python
import jax
import jax.numpy as jnp
from jax import lax
from jax.sharding import PartitionSpec as P


inv_root_two = 0.7071067811865476
inv_root_two_pi = 0.3989422804014327
f32 = jnp.float32
bf16 = jnp.bfloat16


def normal_cdf(value):
    return 0.5 * (1.0 + lax.erf(value * inv_root_two))


def shift_dp(value, flip):
    count = lax.axis_size("dp")
    return lax.ppermute(value, "dp", [(g, g ^ flip) for g in range(count)])


def swap_mp(value, flip):
    count = lax.axis_size("mp")
    return lax.ppermute(value, "mp", [(m, m ^ flip) for m in range(count)])


def sum_mp(value):
    flip = 1
    while flip < lax.axis_size("mp"):
        value = value + swap_mp(value, flip)
        flip *= 2
    return value


def rows_dot(left, right):
    return jnp.dot(left, right, preferred_element_type=f32)


def rows_dot_t(left, right):
    return lax.dot_general(left, right, (((1,), (1,)), ((), ())), preferred_element_type=f32)


def outer_dot(left, right):
    return lax.dot_general(left, right, (((0,), (0,)), ((), ())), preferred_element_type=f32)


def gram(value):
    return rows_dot_t(value, value)


def pick(stack, index):
    return lax.dynamic_index_in_dim(stack, index, 0, keepdims=False)


def spread(block, groups):
    me, count_mp = lax.axis_index("dp"), lax.axis_size("mp")
    if count_mp == 2 * groups:
        core, line = lax.axis_index("mp") % 2, lax.axis_index("mp") // 2

        def at(g, z, c):
            return g * count_mp + 2 * z + c

        found = []
        for flip in range(groups):
            pairs = [
                (at(g, z, c), at(z, g ^ flip, c))
                for g in range(groups)
                for z in range(groups)
                for c in range(2)
            ]
            found.append(lax.ppermute(block, ("dp", "mp"), pairs))
        mine = jnp.stack(found)
        other = swap_mp(mine, 1)
        first = core == 0
        parts = []
        for r in range(groups):
            index = r ^ (line ^ me)
            one, two = pick(mine, index), pick(other, index)
            parts.append(jnp.concatenate([jnp.where(first, one, two), jnp.where(first, two, one)], axis=1))
        return lax.optimization_barrier(parts)
    whole = lax.all_gather(block, "mp", axis=1, tiled=True)
    stack = whole.reshape(whole.shape[0], groups, -1).transpose(1, 0, 2)
    parts = [pick(stack, me ^ flip) for flip in range(groups)]
    return [parts[0]] + [shift_dp(parts[flip], flip) for flip in range(1, groups)]


def reduce_rows(partials, near, far):
    last = near ^ far
    from_near_far = shift_dp(partials[last].astype(bf16), near)
    from_near = shift_dp(partials[near].astype(bf16), near)
    from_far = shift_dp((partials[far] + from_near_far.astype(f32)).astype(bf16), far)
    return partials[0] + from_near.astype(f32) + from_far.astype(f32)


def gather_rows(own, near, far):
    from_near = shift_dp(own, near)
    from_far = shift_dp(own, far)
    from_both = shift_dp(from_near, far)
    found = {0: own, near: from_near, far: from_far, near ^ far: from_both}
    return [found[r] for r in range(4)]


def on_device(inputs, cotangent, w_up, w_down, thresholds):
    groups = lax.axis_size("dp")
    images, patches, feats = inputs.shape
    routes = [(1, 2) if a % 2 == 0 else (2, 1) for a in range(images)]
    image = [slice(a * patches, (a + 1) * patches) for a in range(images)]

    order = (3, 1, 2, 0)

    x_rows, pre = [], []
    for a in range(images):
        x_rows.append(spread(inputs[a], groups))
        partial = {r: rows_dot(x_rows[a][r], w_up) for r in order}
        pre.append(reduce_rows(partial, *routes[a]))

    y_rows = spread(cotangent.reshape(images * patches, feats), groups)
    partial = {r: rows_dot_t(y_rows[r], w_down) for r in order}
    dact = [
        reduce_rows([partial[r][image[a]] for r in range(groups)], *routes[a])
        for a in range(images)
    ]
    own = [inputs[a] for a in range(images)] + [cotangent[a] for a in range(images)]
    grams = sum_mp(jnp.stack([gram(rows) for rows in own]))

    def clip(rows, grams_of, which):
        part = jnp.stack([jnp.sum(grams_of[a] * gram(rows[a])) for a in range(images)])
        norms = jnp.sqrt(sum_mp(part))
        factor = jnp.minimum(1.0, thresholds[which] / (norms + 1e-06))
        return [(factor[a] * rows[a].astype(f32)).astype(bf16) for a in range(images)], norms

    act = [(p * normal_cdf(p)).astype(bf16) for p in pre]
    act_clip, norms_down = clip(act, grams[images:], 1)
    act_rows = [gather_rows(act_clip[a], *routes[a]) for a in range(images)]
    dpre = [
        (d * (normal_cdf(p) + p * jnp.exp(-0.5 * p * p) * inv_root_two_pi)).astype(bf16)
        for p, d in zip(pre, dact)
    ]
    dpre_clip, norms_up = clip(dpre, grams[:images], 0)
    dpre_rows = [gather_rows(dpre_clip[a], *routes[a]) for a in range(images)]

    def flat(wanted):
        return jnp.concatenate(wanted, axis=0)

    def hidden(rows, wanted):
        return flat([rows[a][r] for r in wanted for a in range(images)])

    every, early, late = list(range(groups)), list(range(groups - 1)), [groups - 1]
    grad_down = outer_dot(hidden(act_rows, every), flat(y_rows))
    grad_up = outer_dot(hidden(x_rows, early), hidden(dpre_rows, early))
    grad_up = grad_up + outer_dot(hidden(x_rows, late), hidden(dpre_rows, late))
    return (grad_up, grad_down, jnp.stack([norms_up, norms_down], axis=1))


def solution(mesh):
    assert mesh.shape["dp"] == 4
    in_specs = (P("dp", None, "mp"), P("dp", None, "mp"), P("dp", "mp"), P("mp", "dp"), P())
    out_specs = (P("dp", "mp"), P("mp", "dp"), P("dp", None))

    return jax.shard_map(on_device, mesh=mesh, in_specs=in_specs, out_specs=out_specs, check_vma=False)
```

```python
import jax
import jax.numpy as jnp
from jax import lax
from jax.sharding import PartitionSpec as P


inv_root_two = 0.7071067811865476
inv_root_two_pi = 0.3989422804014327
f32 = jnp.float32
bf16 = jnp.bfloat16


def normal_cdf(value):
    return 0.5 * (1.0 + lax.erf(value * inv_root_two))


def shift_dp(value, flip):
    count = lax.axis_size("dp")
    return lax.ppermute(value, "dp", [(g, g ^ flip) for g in range(count)])


def swap_mp(value, flip):
    count = lax.axis_size("mp")
    return lax.ppermute(value, "mp", [(m, m ^ flip) for m in range(count)])


def sum_mp(value):
    flip = 1
    while flip < lax.axis_size("mp"):
        value = value + swap_mp(value, flip)
        flip *= 2
    return value


def rows_dot(left, right):
    return jnp.dot(left, right, preferred_element_type=f32)


def rows_dot_t(left, right):
    return lax.dot_general(left, right, (((1,), (1,)), ((), ())), preferred_element_type=f32)


def outer_dot(left, right):
    return lax.dot_general(left, right, (((0,), (0,)), ((), ())), preferred_element_type=f32)


def gram(value):
    return rows_dot_t(value, value)


def pick(stack, index):
    return lax.dynamic_index_in_dim(stack, index, 0, keepdims=False)


def spread(block, groups):
    me, count_mp = lax.axis_index("dp"), lax.axis_size("mp")
    if count_mp == 2 * groups:
        core, line = lax.axis_index("mp") % 2, lax.axis_index("mp") // 2

        def at(g, z, c):
            return g * count_mp + 2 * z + c

        found = []
        for flip in range(groups):
            pairs = [
                (at(g, z, c), at(z, g ^ flip, c))
                for g in range(groups)
                for z in range(groups)
                for c in range(2)
            ]
            found.append(lax.ppermute(block, ("dp", "mp"), pairs))
        mine = jnp.stack(found)
        other = swap_mp(mine, 1)
        first = core == 0
        parts = []
        for r in range(groups):
            index = r ^ (line ^ me)
            one, two = pick(mine, index), pick(other, index)
            parts.append(jnp.concatenate([jnp.where(first, one, two), jnp.where(first, two, one)], axis=1))
        return lax.optimization_barrier(parts)
    whole = lax.all_gather(block, "mp", axis=1, tiled=True)
    stack = whole.reshape(whole.shape[0], groups, -1).transpose(1, 0, 2)
    parts = [pick(stack, me ^ flip) for flip in range(groups)]
    return [parts[0]] + [shift_dp(parts[flip], flip) for flip in range(1, groups)]


def reduce_rows(partials, near, far):
    last = near ^ far
    from_near_far = shift_dp(partials[last].astype(bf16), near)
    from_near = shift_dp(partials[near].astype(bf16), near)
    from_far = shift_dp((partials[far] + from_near_far.astype(f32)).astype(bf16), far)
    return partials[0] + from_near.astype(f32) + from_far.astype(f32)


def gather_rows(own, near, far):
    from_near = shift_dp(own, near)
    from_far = shift_dp(own, far)
    from_both = shift_dp(from_near, far)
    found = {0: own, near: from_near, far: from_far, near ^ far: from_both}
    return [found[r] for r in range(4)]


def on_device(inputs, cotangent, w_up, w_down, thresholds):
    groups = lax.axis_size("dp")
    images, patches, feats = inputs.shape
    routes = [(1, 2) if a % 2 == 0 else (2, 1) for a in range(images)]
    image = [slice(a * patches, (a + 1) * patches) for a in range(images)]

    order = (3, 1, 2, 0)

    x_rows, pre = [], []
    for a in range(images):
        x_rows.append(spread(inputs[a], groups))
        partial = {}
        for r in order:
            partial[r] = rows_dot(x_rows[a][r], w_up)
        pre.append(reduce_rows(partial, *routes[a]))

    y_rows = spread(cotangent.reshape(images * patches, feats), groups)
    partial = {}
    for r in order:
        partial[r] = rows_dot_t(y_rows[r], w_down)
    dact = [reduce_rows([partial[r][image[a]] for r in range(groups)], *routes[a]) for a in range(images)]
    own = [inputs[a] for a in range(images)] + [cotangent[a] for a in range(images)]
    grams = sum_mp(jnp.stack([gram(rows) for rows in own]))

    def clip(rows, grams_of, thresholds, which):
        part = jnp.stack([jnp.sum(grams_of[a] * gram(rows[a])) for a in range(images)])
        norms = jnp.sqrt(sum_mp(part))
        factor = jnp.minimum(1.0, thresholds[which] / (norms + 1e-06))
        return [(factor[a] * rows[a].astype(f32)).astype(bf16) for a in range(images)], norms

    act = [(p * normal_cdf(p)).astype(bf16) for p in pre]
    pre, act = lax.optimization_barrier((pre, act))
    act_clip, norms_down = clip(act, grams[images:], thresholds, 1)
    act_rows = [gather_rows(act_clip[a], *routes[a]) for a in range(images)]
    dpre = [
        (d * (normal_cdf(p) + p * jnp.exp(-0.5 * p * p) * inv_root_two_pi)).astype(bf16)
        for p, d in zip(pre, dact)
    ]
    dpre, grams, thresholds, norms_down = lax.optimization_barrier((dpre, grams, thresholds, norms_down))
    dpre_clip, norms_up = clip(dpre, grams[:images], thresholds, 0)
    dpre_rows = [gather_rows(dpre_clip[a], *routes[a]) for a in range(images)]

    def flat(wanted):
        return jnp.concatenate(wanted, axis=0)

    def hidden(rows, wanted):
        return flat([rows[a][r] for r in wanted for a in range(images)])

    every, early, late = list(range(groups)), list(range(groups - 1)), [groups - 1]
    grad_down = outer_dot(hidden(act_rows, every), flat(y_rows))
    grad_up = outer_dot(hidden(x_rows, early), hidden(dpre_rows, early))
    grad_up = grad_up + outer_dot(hidden(x_rows, late), hidden(dpre_rows, late))
    return (grad_up, grad_down, jnp.stack([norms_up, norms_down], axis=1))


def solution(mesh):
    assert mesh.shape["dp"] == 4
    in_specs = (P("dp", None, "mp"), P("dp", None, "mp"), P("dp", "mp"), P("mp", "dp"), P())
    out_specs = (P("dp", "mp"), P("mp", "dp"), P("dp", None))

    return jax.shard_map(on_device, mesh=mesh, in_specs=in_specs, out_specs=out_specs, check_vma=False)
```
